32 devices in a mesh: fsdp: 2 (over x), ctx: 4 (over y, core), tp: 4 (over z).
Axes of the slice: x: 2, y: 2, z: 4, core: 2. Of those that a mesh axis runs over, the one named last changes fastest.
Arguments:
- tokens: bfloat16 [2, 1152, 1024], P('fsdp', 'ctx'), may hold values from -6 to 6
- segment_ids: int32 [2, 1152], P('fsdp'), may hold values from 0 to 2, never falling along the last dimension, each value on 1 to 576 neighbouring positions
- first_gain: bfloat16 [1024], P(('fsdp', 'ctx')), may hold values from 0.5 to 1.5
- first_shift: bfloat16 [1024], P(('fsdp', 'ctx')), may hold values from -3 to 3
- input_weight: bfloat16 [3, 1024, 1024], P(None, ('fsdp', 'ctx'), 'tp'), may hold values from -0.1875 to 0.1875
- input_bias: bfloat16 [2, 1024], P(None, 'tp'), may hold values from -3 to 3
- output_weight: bfloat16 [1024, 1024], P('tp', ('fsdp', 'ctx')), may hold values from -0.75 to 0.75
- output_bias: bfloat16 [1024], P(('fsdp', 'ctx')), may hold values from -3 to 3
- second_gain: bfloat16 [1024], P(('fsdp', 'ctx')), may hold values from 0.5 to 1.5
- second_shift: bfloat16 [1024], P(('fsdp', 'ctx')), may hold values from -3 to 3
- up_weight: bfloat16 [1024, 4096], P(('fsdp', 'ctx'), 'tp'), may hold values from -0.1875 to 0.1875
- up_bias: bfloat16 [4096], P('tp'), may hold values from -3 to 3
- down_weight: bfloat16 [4096, 1024], P('tp', ('fsdp', 'ctx')), may hold values from -0.125 to 0.125
- down_bias: bfloat16 [1024], P(('fsdp', 'ctx')), may hold values from -3 to 3
- cotangent: bfloat16 [2, 1152, 1024], P('fsdp', 'ctx'), may hold values from -6 to 6
Outputs:
- result: bfloat16 [2, 1152, 1024], P('fsdp', 'ctx')
- tokens_grad: float32 [2, 1152, 1024], P('fsdp', 'ctx')
- first_gain_grad: float32 [1024], P(('fsdp', 'ctx'))
- first_shift_grad: float32 [1024], P(('fsdp', 'ctx'))
- input_weight_grad: float32 [3, 1024, 1024], P(None, ('fsdp', 'ctx'), 'tp')
- input_bias_grad: float32 [2, 1024], P(None, 'tp')
- output_weight_grad: float32 [1024, 1024], P('tp', ('fsdp', 'ctx'))
- output_bias_grad: float32 [1024], P(('fsdp', 'ctx'))
- second_gain_grad: float32 [1024], P(('fsdp', 'ctx'))
- second_shift_grad: float32 [1024], P(('fsdp', 'ctx'))
- up_weight_grad: float32 [1024, 4096], P(('fsdp', 'ctx'), 'tp')
- up_bias_grad: float32 [4096], P('tp')
- down_weight_grad: float32 [4096, 1024], P('tp', ('fsdp', 'ctx'))
- down_bias_grad: float32 [1024], P(('fsdp', 'ctx'))
The draws below stay inside these ranges and needn't reach their ends.
Inputs may be any that keep to these rules, and one draw needn't show every extreme that they name: `segment_ids`: along each sequence the ids never fall; each id covers 1 to 576 consecutive positions.
All inputs are finite; a program needn't handle non-finite values.
Results may differ from the reference program's by a relative error of at most 0.017.
Values may be sent and summed in bfloat16 or wider, within the bound.
No kernel may reach another device: no remote copies, remote signals or barrier semaphores. Data moves between devices by JAX's collectives and lax.ppermute only.
A program may use at most 128 MiB of HBM per device.

```python
import math
import jax
import jax.numpy as jnp
import numpy as np
from jax import lax

D = 1024
HEADS = 16
HEAD_DIM = 64
FF = 4096
LEN = 1152
SEQS = 2


def block_levels(key, extent, shards, low, high):
    level, own = 1.0, jax.random.fold_in(key, 6)
    for position, shards_of in shards:
        steps = jnp.exp(jax.random.uniform(jax.random.fold_in(own, position), (shards_of,), jnp.float32, low / len(shards), high / len(shards)))
        level = level * jnp.repeat(steps, extent[position] // shards_of).reshape([-1 if axis == position else 1 for axis in range(len(extent))])
    return level


def split_up(count, total, limit, skew):
    loads = [(1 << 20) // math.isqrt(standing ** skew) + 1 for standing in range(2, count + 1)]
    spare, given = total - limit - (count - 1), [1] * (count - 1)
    while spare > 0:
        movable = [i for i in range(count - 1) if given[i] < limit]
        mass, budget = sum([loads[i] for i in movable]), spare
        for i in movable:
            addition = min(limit - given[i], max(1, budget * loads[i] // mass), spare)
            given[i] = given[i] + addition
            spare = spare - addition
    return np.array([limit] + given)


def uneven(rng, number_of, total, limit, skew):
    if number_of == 2:
        one = jax.random.randint(rng, (), max(1, total - limit), min(limit, total - 1) + 1)
        return jnp.stack([one, total - one])
    tallies = jnp.asarray(split_up(number_of, total, limit, skew), jnp.int32)
    pairs = (number_of - 1) // 2
    source_of, sink = tallies[1:1 + 2 * pairs:2], tallies[2:2 + 2 * pairs:2]
    margin = jnp.minimum(source_of - 1, limit - sink)
    shifted = jax.random.randint(jax.random.fold_in(rng, 1), (pairs,), 0, 1 << 20) % (margin + 1)
    tallies = tallies.at[1:1 + 2 * pairs:2].set(source_of - shifted).at[2:2 + 2 * pairs:2].set(sink + shifted)
    return tallies[jax.random.permutation(jax.random.fold_in(rng, 2), number_of)]


def gaussian(rng, extent, scale, bound, pieces=(), held_as=jnp.bfloat16):
    drawn = scale * jax.random.normal(rng, extent, jnp.float32)
    if pieces:
        drawn = drawn * block_levels(rng, extent, pieces, -0.22, 0.18)
    return jnp.clip(drawn, -bound, bound).astype(held_as)


def setup_inputs(seed: int = 0) -> dict:
    keys = jax.random.split(jax.random.key(seed), 16)
    tokens = gaussian(keys[0], (SEQS, LEN, D), 1.0, 6.0, ((0, 2), (1, 4)))
    segment_ids = jax.vmap(lambda own: jnp.searchsorted(jnp.cumsum(uneven(own, 3, LEN, LEN // 2, 0)), jnp.arange(LEN), side="right"))(jax.random.split(keys[1], SEQS)).reshape((SEQS, LEN)).astype(jnp.int32)
    first_gain = jnp.clip(1.0 + 0.1 * jax.random.normal(keys[2], (D,), jnp.float32), 0.5, 1.5).astype(jnp.bfloat16)
    first_shift = gaussian(keys[3], (D,), 0.3, 3.0, ((0, 8),))
    input_weight = gaussian(keys[4], (3, D, D), D ** -0.5, 0.1875, ((1, 8), (2, 4)))
    input_bias = gaussian(keys[5], (2, D), 0.5, 3.0, ((1, 4),))
    output_weight = gaussian(keys[6], (D, D), (D // 16) ** -0.5, 0.75, ((0, 4), (1, 8)))
    output_bias = gaussian(keys[7], (D,), 0.5, 3.0, ((0, 8),))
    second_gain = jnp.clip(1.0 + 0.1 * jax.random.normal(keys[8], (D,), jnp.float32), 0.5, 1.5).astype(jnp.bfloat16)
    second_shift = gaussian(keys[9], (D,), 0.3, 3.0, ((0, 8),))
    up_weight = gaussian(keys[10], (D, FF), D ** -0.5, 0.1875, ((0, 8), (1, 4)))
    up_bias = gaussian(keys[11], (FF,), 0.5, 3.0, ((0, 4),))
    down_weight = gaussian(keys[12], (FF, D), (FF // 2) ** -0.5, 0.125, ((0, 4), (1, 8)))
    down_bias = gaussian(keys[13], (D,), 0.5, 3.0, ((0, 8),))
    cotangent = gaussian(keys[14], (SEQS, LEN, D), 1.0, 6.0, ((0, 2), (1, 4)))
    return {"tokens": tokens, "segment_ids": segment_ids, "first_gain": first_gain, "first_shift": first_shift, "input_weight": input_weight, "input_bias": input_bias, "output_weight": output_weight, "output_bias": output_bias, "second_gain": second_gain, "second_shift": second_shift, "up_weight": up_weight, "up_bias": up_bias, "down_weight": down_weight, "down_bias": down_bias, "cotangent": cotangent}


@jax.custom_vjp
def low(v):
    return lax.optimization_barrier(v.astype(jnp.bfloat16)).astype(jnp.float32)

@jax.custom_vjp
def low_back(v):
    return v

def low_keep(v):
    return (low(v), None)

def low_pass(kept, grad):
    return (grad,)

def back_keep(v):
    return (v, None)

def back_low(kept, grad):
    return (low(grad),)
low.defvjp(low_keep, low_pass)
low_back.defvjp(back_keep, back_low)
EPSILON = 1e-05

def layer_norm(values_in, gain, shift):
    center = values_in - lax.optimization_barrier(jnp.mean(values_in, axis=-1, keepdims=True))
    spread = lax.optimization_barrier(jnp.mean(center * center, axis=-1, keepdims=True))
    return center * lax.rsqrt(spread + EPSILON) * gain + shift

def forward_layer(seq_tokens, seq_segments, first_gain, first_shift, input_weight, input_bias, output_weight, output_bias, second_gain, second_shift, up_weight, up_bias, down_weight, down_bias):
    highest = lax.Precision.HIGHEST
    seq_length = seq_tokens.shape[0]
    normed_one = low(layer_norm(seq_tokens, first_gain, first_shift))
    projected = jnp.einsum('ld,jde->jle', normed_one, input_weight, precision=highest)
    queries = low(low_back(projected[0] + input_bias[0]))
    keys_all = low(low_back(projected[1]))
    values_all = low(low_back(projected[2] + input_bias[1]))
    query_heads = queries.reshape(seq_length, HEADS, HEAD_DIM)
    key_heads = keys_all.reshape(seq_length, HEADS, HEAD_DIM)
    value_heads = values_all.reshape(seq_length, HEADS, HEAD_DIM)
    score_scale = 1.0 / math.sqrt(HEAD_DIM)
    scores = jnp.einsum('qhc,khc->hqk', query_heads, key_heads, precision=highest) * score_scale
    scores = low_back(scores)
    positions = jnp.arange(seq_length, dtype=jnp.int32)
    allowed_here = (seq_segments[:, None] == seq_segments[None, :]) & (positions[None, :] <= positions[:, None])
    probs = jax.nn.softmax(jnp.where(allowed_here[None], scores, -1e+30), axis=-1)
    probs = low(probs)
    mixed_heads = jnp.einsum('hqk,khc->qhc', probs, value_heads, precision=highest)
    mixed_heads = low(low_back(mixed_heads.reshape(seq_length, HEADS * HEAD_DIM)))
    attn_out = low_back(jnp.dot(mixed_heads, output_weight, precision=highest) + output_bias)
    middle = seq_tokens + attn_out
    normed_two = low(layer_norm(middle, second_gain, second_shift))
    hidden = low_back(jnp.dot(normed_two, up_weight, precision=highest) + up_bias)
    active = low(jax.nn.gelu(hidden, approximate=True))
    mlp_out = jnp.dot(active, down_weight, precision=highest) + down_bias
    return middle + mlp_out

def reference(tokens, segment_ids, first_gain, first_shift, input_weight, input_bias, output_weight, output_bias, second_gain, second_shift, up_weight, up_bias, down_weight, down_bias, cotangent):
    params = tuple((weight.astype(jnp.float32) for weight in (first_gain, first_shift, input_weight, input_bias, output_weight, output_bias, second_gain, second_shift, up_weight, up_bias, down_weight, down_bias)))
    starting = tuple((jnp.zeros_like(weight) for weight in params))

    def one_sequence(totals, inputs):
        seq_tokens, seq_segments, seq_cot = inputs

        def run_layer(seq_in, *weights):
            return forward_layer(seq_in, seq_segments, *weights)
        outputs, pullback = jax.vjp(run_layer, seq_tokens.astype(jnp.float32), *params)
        gradients = pullback(seq_cot.astype(jnp.float32))
        totals = tuple((older + newer for older, newer in zip(totals, gradients[1:])))
        return (totals, (outputs.astype(jnp.bfloat16), gradients[0]))
    totals, (result, tokens_grad) = lax.scan(one_sequence, starting, (tokens, segment_ids, cotangent))
    return (result, tokens_grad, totals[0], totals[1], totals[2], totals[3], totals[4], totals[5], totals[6], totals[7], totals[8], totals[9], totals[10], totals[11])
```

```python
from functools import partial
import math

import jax
import jax.numpy as jnp
from jax import lax
from jax.experimental import pallas as pl
from jax.experimental.pallas import tpu as pltpu
from jax.sharding import PartitionSpec as P

HEADS = 16
HEAD_DIM = 64
MAX_SEGMENT = 576
EPSILON = 1e-05
FC = ("fsdp", "ctx")
BF = jnp.bfloat16
F32 = jnp.float32


def gate(value, after):
    return lax.optimization_barrier((value, after))[0]


def swap(x, axis, offset):
    size = lax.axis_size(axis)
    return lax.ppermute(x, axis, [(i, i ^ offset) for i in range(size)])


def order(size):
    return [2 * i for i in range(size // 2)] + [2 * i + 1 for i in range(size // 2)]


def place_of(offset, size):
    return (offset & 1) * (size // 2) + (offset >> 1)


def device_index():
    return lax.axis_index("fsdp") * lax.axis_size("ctx") + lax.axis_index("ctx")


def group_size():
    return lax.axis_size("fsdp") * lax.axis_size("ctx")


def to_relative(x):
    size, me = group_size(), device_index()
    width = x.shape[1] // size
    return jnp.concatenate(
        [lax.dynamic_slice_in_dim(x, (me ^ o) * width, width, 1) for o in order(size)], axis=1
    )


def to_absolute(x):
    size, me = group_size(), device_index()
    width = x.shape[1] // size
    return jnp.concatenate(
        [
            lax.dynamic_slice_in_dim(x, place_of(me ^ j, size) * width, width, 1)
            for j in range(size)
        ],
        axis=1,
    )


def gather_pieces(w):
    size = group_size()
    if size > 8:
        picked = jnp.take(
            lax.all_gather(w, FC), device_index() ^ jnp.array(order(size)), axis=0
        )
        return [picked[i] for i in range(size)]
    evens = [w] + [swap(w, FC, o) for o in order(size)[1 : size // 2]]
    return evens + [swap(piece, FC, 1) for piece in evens]


def scatter_sum(even, odd, axis):
    size = group_size()
    half = size // 2
    if size > 8:
        pieces = jnp.stack(jnp.split(even, half, axis) + jnp.split(odd, half, axis)).astype(BF)
        wanted = place_of(device_index() ^ jnp.arange(size), size)
        parts = lax.all_to_all(jnp.take(pieces, wanted, axis=0), FC, 0, 0, tiled=True)
        return jnp.sum(parts.astype(F32), axis=0)
    summed = even.astype(F32) + swap(odd.astype(BF), FC, 1).astype(F32)
    pieces = jnp.split(summed, half, axis)
    total = pieces[0]
    for o, piece in zip(order(size)[1:half], pieces[1:]):
        total = total + swap(piece.astype(BF), FC, o).astype(F32)
    return total


def sum_all(x, axis, size):
    step = 1
    while step < size:
        x = x + swap(x, axis, step)
        step *= 2
    return x


def row_block(x, index, rows):
    return lax.dynamic_slice_in_dim(x, index * rows, rows, 0)


def tp_scatter_rows(partial_sum):
    tp, t = lax.axis_size("tp"), lax.axis_index("tp")
    rows = partial_sum.shape[0] // tp
    total = row_block(partial_sum, t, rows)
    for s in range(1, tp):
        total = total + swap(row_block(partial_sum, t ^ s, rows).astype(BF), "tp", s).astype(F32)
    return total


def put_rows(pieces):
    tp, t = lax.axis_size("tp"), lax.axis_index("tp")
    rows = pieces[0].shape[0]
    out = jnp.zeros((rows * tp, pieces[0].shape[1]), pieces[0].dtype)
    for s, piece in enumerate(pieces):
        out = lax.dynamic_update_slice_in_dim(out, piece, (t ^ s) * rows, 0)
    return out


def tp_gather_rows(x, dtype):
    tp = lax.axis_size("tp")
    pieces = [x] + [swap(x, "tp", s) for s in range(1, tp)]
    return put_rows([piece.astype(dtype) for piece in pieces])


def normalise(x):
    center = x - jnp.mean(x, axis=-1, keepdims=True)
    inverse = lax.rsqrt(jnp.mean(center * center, axis=-1, keepdims=True) + EPSILON)
    return center * inverse, inverse


def normalise_back(grad, gain, xhat, inverse):
    gx = grad * gain
    mean_gx = jnp.mean(gx, axis=-1, keepdims=True)
    mean_gxx = jnp.mean(gx * xhat, axis=-1, keepdims=True)
    return (gx - mean_gx - xhat * mean_gxx) * inverse


def nt(a, b):
    return lax.dot_general(a, b, (((1,), (1,)), ((), ())), preferred_element_type=F32)


def tn(a, b):
    return lax.dot_general(a, b, (((0,), (0,)), ((), ())), preferred_element_type=F32)


def attend_kernel(blocks, *refs):
    q_ref, bias_ref = refs[0], refs[1]
    k_refs, v_refs = refs[2 : 2 + blocks], refs[2 + blocks : 2 + 2 * blocks]
    out_ref, total_ref = refs[2 + 2 * blocks :]
    rows = q_ref.shape[0]
    for h in range(q_ref.shape[1] // HEAD_DIM):
        cols = slice(h * HEAD_DIM, (h + 1) * HEAD_DIM)
        q = q_ref[:, cols]
        scores = [
            nt(k_refs[b][:, cols], q) + bias_ref[b * rows : (b + 1) * rows, :]
            for b in range(blocks)
        ]
        highest = scores[0].max(axis=0, keepdims=True)
        for s in scores[1:]:
            highest = jnp.maximum(highest, s.max(axis=0, keepdims=True))
        weights = [jnp.exp(s - highest) for s in scores]
        summed = sum(w.sum(axis=0, keepdims=True) for w in weights)
        scale = 1.0 / summed
        mixed = sum(
            tn(v_refs[b][:, cols], (weights[b] * scale).astype(BF)) for b in range(blocks)
        )
        out_ref[:, cols] = mixed.T.astype(BF)
        total_ref[0, h : h + 1, :] = highest + jnp.log(summed)


def attend_back_kernel(blocks, *refs):
    q_ref, grad_ref, bias_ref, total_ref = refs[:4]
    k_refs, v_refs = refs[4 : 4 + blocks], refs[4 + blocks : 4 + 2 * blocks]
    outs = refs[4 + 2 * blocks :]
    gq_ref, gk_refs, gv_refs = outs[0], outs[1 : 1 + blocks], outs[1 + blocks :]
    rows = q_ref.shape[0]
    for h in range(q_ref.shape[1] // HEAD_DIM):
        cols = slice(h * HEAD_DIM, (h + 1) * HEAD_DIM)
        q, grad = q_ref[:, cols], grad_ref[:, cols]
        total = total_ref[0, h : h + 1, :]
        probs, grads = [], []
        for b in range(blocks):
            s = nt(k_refs[b][:, cols], q) + bias_ref[b * rows : (b + 1) * rows, :]
            probs.append(jnp.exp(s - total))
            grads.append(nt(v_refs[b][:, cols], grad))
        inner = sum((p * g).sum(axis=0, keepdims=True) for p, g in zip(probs, grads))
        gq = None
        for b in range(blocks):
            gs = (probs[b] * (grads[b] - inner)).astype(BF)
            gk = jnp.dot(gs, q, preferred_element_type=F32)
            gv = jnp.dot(probs[b].astype(BF), grad, preferred_element_type=F32)
            gk_refs[b][:, cols] = gk.astype(gk_refs[b].dtype)
            gv_refs[b][:, cols] = gv.astype(gv_refs[b].dtype)
            part = tn(k_refs[b][:, cols], gs)
            gq = part if gq is None else gq + part
        gq_ref[:, cols] = (gq.T * (1.0 / math.sqrt(HEAD_DIM))).astype(gq_ref.dtype)


def attention_specs(rows, width, blocks):
    pair = 2 * HEAD_DIM
    steps = width // pair
    tile = pl.BlockSpec((rows, pair), lambda j: (0, j))
    value_tile = pl.BlockSpec((rows, pair), lambda j: (0, steps + j))
    bias = pl.BlockSpec((blocks * rows, rows), lambda j: (0, 0))
    total = pl.BlockSpec((1, 2, rows), lambda j: (j, 0, 0))
    return steps, tile, value_tile, bias, total


def attend(q, kv, bias):
    rows, width = q.shape
    blocks = len(kv)
    steps, tile, value_tile, bias_spec, total = attention_specs(rows, width, blocks)
    return pl.pallas_call(
        partial(attend_kernel, blocks),
        grid=(steps,),
        in_specs=[tile, bias_spec] + [tile] * blocks + [value_tile] * blocks,
        out_specs=[tile, total],
        out_shape=[
            jax.ShapeDtypeStruct((rows, width), BF),
            jax.ShapeDtypeStruct((steps, 2, rows), F32),
        ],
        cost_estimate=pl.CostEstimate(
            flops=4 * blocks * rows * rows * width,
            bytes_accessed=4 * blocks * rows * (rows + width),
            transcendentals=blocks * rows * rows * width // HEAD_DIM,
        ),
        name="attend",
    )(q, bias, *kv, *kv)


def attend_back(q, kv, bias, totals, grad):
    rows, width = q.shape
    blocks = len(kv)
    steps, tile, value_tile, bias_spec, total = attention_specs(rows, width, blocks)
    kinds = [F32] + [BF] * (blocks - 1)
    return pl.pallas_call(
        partial(attend_back_kernel, blocks),
        grid=(steps,),
        in_specs=[tile, tile, bias_spec, total] + [tile] * blocks + [value_tile] * blocks,
        out_specs=[tile] * (1 + 2 * blocks),
        out_shape=[jax.ShapeDtypeStruct((rows, width), k) for k in [BF] + kinds + kinds],
        cost_estimate=pl.CostEstimate(
            flops=10 * blocks * rows * rows * width,
            bytes_accessed=4 * blocks * rows * (rows + width),
            transcendentals=blocks * rows * rows * width // HEAD_DIM,
        ),
        name="attend_back",
    )(q, grad, bias, totals, *kv, *kv)


def local(
    tokens,
    segment_ids,
    first_gain,
    first_shift,
    input_weight,
    input_bias,
    output_weight,
    output_bias,
    second_gain,
    second_shift,
    up_weight,
    up_bias,
    down_weight,
    down_bias,
    cotangent,
):
    sequences, rows, features = tokens.shape
    ctx, tp = lax.axis_size("ctx"), lax.axis_size("tp")
    c, t = lax.axis_index("ctx"), lax.axis_index("tp")
    size = group_size()
    half = features // 2
    chunk = rows // tp
    width = input_weight.shape[2]
    earlier = min(ctx - 1, -(-(MAX_SEGMENT - 1) // rows))
    blocks = earlier + 1

    vectors = jnp.stack(
        [first_gain, first_shift, output_bias, second_gain, second_shift, down_bias]
    )
    in_pieces = gather_pieces(input_weight)
    vector_pieces = gather_pieces(vectors)
    vectors_full = jnp.concatenate(vector_pieces, axis=1).astype(F32)
    gain_one, shift_one, out_shift, gain_two, shift_two, down_shift = [
        vectors_full[i : i + 1] for i in range(6)
    ]
    out_rows = jnp.concatenate(
        [output_weight] + [swap(output_weight, "tp", s) for s in range(1, tp)], axis=0
    )

    resid = to_relative(tokens.reshape(rows, features)).astype(F32)
    cot_low = to_relative(cotangent.reshape(rows, features))
    xhat_one, inverse_one = normalise(resid)
    normed_low = (xhat_one * gain_one + shift_one).astype(BF)

    ids = segment_ids.reshape(-1)
    query_seg = lax.dynamic_slice_in_dim(ids, c * rows, rows, 0)
    padded = jnp.concatenate([jnp.full((earlier * rows,), -1, ids.dtype), ids])
    biases = []
    for b in range(blocks):
        key_seg = lax.dynamic_slice_in_dim(padded, (c + earlier - b) * rows, rows, 0)
        allowed = key_seg[:, None] == query_seg[None, :]
        if b == 0:
            place = jnp.arange(rows)
            allowed = allowed & (place[:, None] <= place[None, :])
        biases.append(jnp.where(allowed, 0.0, -1e30).astype(F32))
    bias = jnp.concatenate(biases, axis=0)

    in_full = jnp.concatenate(in_pieces, axis=1)
    query_part = jnp.dot(normed_low, in_full[0], preferred_element_type=F32)
    key_part = jnp.dot(normed_low, in_full[1], preferred_element_type=F32)
    value_part = jnp.dot(normed_low, in_full[2], preferred_element_type=F32)
    queries = (query_part + input_bias[0].astype(F32)).astype(BF)
    queries = queries * jnp.asarray(1.0 / math.sqrt(HEAD_DIM), BF)
    values = (value_part + input_bias[1].astype(F32)).astype(BF)
    kv = [jnp.concatenate([key_part.astype(BF), values], axis=1)]
    for b in range(1, blocks):
        kv.append(lax.ppermute(kv[0], "ctx", [(i, i + b) for i in range(ctx - b)]))

    out_pieces = gather_pieces(gate(out_rows, in_pieces[-1]))
    up_local, down_local = gate((up_weight, down_weight), kv[-1])
    up_pieces = gather_pieces(up_local)
    down_pieces = gather_pieces(down_local)

    mixed, totals = attend(queries, kv, bias)
    mixed_all = jnp.concatenate(
        [mixed] + [swap(mixed, "tp", s) for s in range(1, tp)], axis=1
    )
    out_full = jnp.concatenate(out_pieces, axis=1)
    middle = resid + out_shift + jnp.dot(mixed_all, out_full, preferred_element_type=F32)
    xhat_two, inverse_two = normalise(middle)
    normed_two = (xhat_two * gain_two + shift_two).astype(BF)
    up_full = jnp.concatenate(up_pieces, axis=0)
    down_full = jnp.concatenate(down_pieces, axis=1)
    hidden = jnp.dot(normed_two, up_full, preferred_element_type=F32) + up_bias.astype(F32)
    gelu_tanh = partial(jax.nn.gelu, approximate=True)
    active, gelu_pullback = jax.vjp(gelu_tanh, hidden)
    active = active.astype(BF)
    grad_active = nt(cot_low, down_full)
    grad_hidden = gelu_pullback(grad_active)[0].astype(BF)
    grad_norm_two = tp_scatter_rows(nt(grad_hidden, up_full))

    middle_rows = row_block(middle, t, chunk)
    xhat_rows, inverse_rows = row_block(xhat_two, t, chunk), row_block(inverse_two, t, chunk)
    cot_rows = row_block(cot_low, t, chunk).astype(F32)
    grad_middle = cot_rows + normalise_back(grad_norm_two, gain_two, xhat_rows, inverse_rows)
    grad_attn = grad_middle.astype(BF)
    grad_mixed = nt(grad_attn, out_full).astype(BF)
    grad_pieces = jnp.split(grad_mixed, tp, axis=1)
    grad_heads = put_rows(
        [grad_pieces[0]] + [swap(grad_pieces[s], "tp", s) for s in range(1, tp)]
    )

    grad_up_odd = tn(normed_two[:, half:], grad_hidden).astype(BF)
    grad_up_even = tn(normed_two[:, :half], grad_hidden)
    grad_down_odd = tn(active, cot_low[:, half:]).astype(BF)
    grad_down_even = tn(active, cot_low[:, :half])
    up_grad = scatter_sum(grad_up_even, grad_up_odd, 0)
    down_grad = scatter_sum(grad_down_even, grad_down_odd, 1)
    grad_up_bias = jnp.sum(grad_hidden.astype(F32), axis=0)

    late_active = gate(active, grad_heads)
    mlp_part = jnp.dot(late_active, down_full, preferred_element_type=F32)
    result_rows = middle_rows + tp_scatter_rows(mlp_part) + down_shift
    result = tp_gather_rows(to_absolute(result_rows.astype(BF)), BF)

    grads = attend_back(queries, kv, bias, totals, grad_heads)
    grad_queries = grads[0]
    grad_keys, grad_values = grads[1], grads[1 + blocks]
    for b in range(1, blocks):
        back = [(i + b, i) for i in range(ctx - b)]
        grad_keys = grad_keys + lax.ppermute(grads[1 + b], "ctx", back).astype(F32)
        grad_values = grad_values + lax.ppermute(grads[1 + blocks + b], "ctx", back).astype(F32)
    grad_three = [grad_queries, grad_keys.astype(BF), grad_values.astype(BF)]
    grad_joined = jnp.concatenate(grad_three, axis=1)

    mixed_rows = row_block(mixed_all, t, chunk)
    out_grad = scatter_sum(
        tn(mixed_rows, grad_attn[:, :half]), tn(mixed_rows, grad_attn[:, half:]), 1
    )
    out_blocks = jnp.split(out_grad, tp, axis=0)
    out_weight_grad = out_blocks[0]
    for s in range(1, tp):
        out_weight_grad = out_weight_grad + swap(out_blocks[s].astype(BF), "tp", s).astype(F32)

    in_joined = jnp.concatenate([in_full[0], in_full[1], in_full[2]], axis=1)
    grad_norm_one = tp_scatter_rows(nt(grad_joined, in_joined))
    in_even = tn(normed_low[:, :half], grad_joined)
    in_odd = tn(normed_low[:, half:], grad_joined)
    in_grad = scatter_sum(in_even, in_odd, 0)
    in_weight_grad = jnp.stack([in_grad[:, i * width : (i + 1) * width] for i in range(3)])
    grad_in_bias = jnp.concatenate(
        [
            jnp.sum(grad_three[0].astype(F32), axis=0),
            jnp.sum(grad_three[2].astype(F32), axis=0),
        ]
    )
    bias_sums = sum_all(jnp.concatenate([grad_in_bias, grad_up_bias])[None, :], FC, size)[0]

    xhat_one_rows = row_block(xhat_one, t, chunk)
    inverse_one_rows = row_block(inverse_one, t, chunk)
    tokens_grad_rows = grad_middle + normalise_back(
        grad_norm_one, gain_one, xhat_one_rows, inverse_one_rows
    )
    tokens_grad = tp_gather_rows(to_absolute(tokens_grad_rows.astype(BF)), F32)

    sums = jnp.stack(
        [
            jnp.sum(grad_norm_one * xhat_one_rows, axis=0),
            jnp.sum(grad_norm_one, axis=0),
            jnp.sum(grad_attn.astype(F32), axis=0),
            jnp.sum(grad_norm_two * xhat_rows, axis=0),
            jnp.sum(grad_norm_two, axis=0),
            jnp.sum(cot_rows, axis=0),
        ]
    )
    sums = sum_all(sums, "tp", tp)
    vector_grads = scatter_sum(sums[:, :half], sums[:, half:], 1)
    return (
        result.reshape(sequences, rows, features),
        tokens_grad.reshape(sequences, rows, features),
        vector_grads[0],
        vector_grads[1],
        in_weight_grad,
        bias_sums[: 2 * width].reshape(2, width),
        out_weight_grad,
        vector_grads[2],
        vector_grads[3],
        vector_grads[4],
        up_grad,
        bias_sums[2 * width :],
        down_grad,
        vector_grads[5],
    )


def solution(mesh):
    in_specs = (
        P("fsdp", "ctx", None),
        P("fsdp", None),
        P(("fsdp", "ctx")),
        P(("fsdp", "ctx")),
        P(None, ("fsdp", "ctx"), "tp"),
        P(None, "tp"),
        P("tp", ("fsdp", "ctx")),
        P(("fsdp", "ctx")),
        P(("fsdp", "ctx")),
        P(("fsdp", "ctx")),
        P(("fsdp", "ctx"), "tp"),
        P("tp"),
        P("tp", ("fsdp", "ctx")),
        P(("fsdp", "ctx")),
        P("fsdp", "ctx", None),
    )
    out_specs = (
        P("fsdp", "ctx", None),
        P("fsdp", "ctx", None),
        P(("fsdp", "ctx")),
        P(("fsdp", "ctx")),
        P(None, ("fsdp", "ctx"), "tp"),
        P(None, "tp"),
        P("tp", ("fsdp", "ctx")),
        P(("fsdp", "ctx")),
        P(("fsdp", "ctx")),
        P(("fsdp", "ctx")),
        P(("fsdp", "ctx"), "tp"),
        P("tp"),
        P("tp", ("fsdp", "ctx")),
        P(("fsdp", "ctx")),
    )
    return jax.shard_map(local, mesh=mesh, in_specs=in_specs, out_specs=out_specs, check_vma=False)
```

```python
from functools import partial
import math

import jax
import jax.numpy as jnp
from jax import lax
from jax.experimental import pallas as pl
from jax.experimental.pallas import tpu as pltpu
from jax.sharding import PartitionSpec as P

HEADS = 16
HEAD_DIM = 64
MAX_SEGMENT = 576
EPSILON = 1e-05
FC = ("fsdp", "ctx")
BF = jnp.bfloat16
F32 = jnp.float32


def gate(value, after):
    return lax.optimization_barrier((value, after))[0]


def swap(x, axis, offset):
    size = lax.axis_size(axis)
    return lax.ppermute(x, axis, [(i, i ^ offset) for i in range(size)])


def order(size):
    return [2 * i for i in range(size // 2)] + [2 * i + 1 for i in range(size // 2)]


def place_of(offset, size):
    return (offset & 1) * (size // 2) + (offset >> 1)


def device_index():
    return lax.axis_index("fsdp") * lax.axis_size("ctx") + lax.axis_index("ctx")


def group_size():
    return lax.axis_size("fsdp") * lax.axis_size("ctx")


def to_relative(x):
    size, me = group_size(), device_index()
    width = x.shape[1] // size
    return jnp.concatenate(
        [lax.dynamic_slice_in_dim(x, (me ^ o) * width, width, 1) for o in order(size)], axis=1
    )


def to_absolute(x):
    size, me = group_size(), device_index()
    width = x.shape[1] // size
    return jnp.concatenate(
        [
            lax.dynamic_slice_in_dim(x, place_of(me ^ j, size) * width, width, 1)
            for j in range(size)
        ],
        axis=1,
    )


def join_kernel(*refs):
    out_ref = refs[-1]
    width = refs[0].shape[1]
    for i, ref in enumerate(refs[:-1]):
        out_ref[:, i * width : (i + 1) * width] = ref[...]


def join(pieces):
    rows, width = pieces[0].shape
    tile = max(d for d in range(16, min(rows, 256) + 1, 16) if rows % d == 0)
    total = width * len(pieces)
    return pl.pallas_call(
        join_kernel,
        grid=(rows // tile,),
        in_specs=[pl.BlockSpec((tile, width), lambda i: (i, 0))] * len(pieces),
        out_specs=pl.BlockSpec((tile, total), lambda i: (i, 0)),
        out_shape=jax.ShapeDtypeStruct((rows, total), pieces[0].dtype),
        cost_estimate=pl.CostEstimate(
            flops=0, bytes_accessed=4 * rows * total, transcendentals=0
        ),
        name="join",
    )(*pieces)


def gather_columns(w):
    size = group_size()
    if size > 8:
        picked = jnp.take(
            lax.all_gather(w, FC), device_index() ^ jnp.array(order(size)), axis=0
        )
        return jnp.moveaxis(picked, 0, 1).reshape(w.shape[0], -1), picked
    even = join([w] + [swap(w, FC, o) for o in order(size)[1 : size // 2]])
    return join([even, swap(even, FC, 1)]), even


def scatter_sum(even, odd, axis):
    size = group_size()
    half = size // 2
    if size > 8:
        pieces = jnp.stack(jnp.split(even, half, axis) + jnp.split(odd, half, axis)).astype(BF)
        wanted = place_of(device_index() ^ jnp.arange(size), size)
        parts = lax.all_to_all(jnp.take(pieces, wanted, axis=0), FC, 0, 0, tiled=True)
        return jnp.sum(parts.astype(F32), axis=0)
    summed = even.astype(F32) + swap(odd.astype(BF), FC, 1).astype(F32)
    pieces = jnp.split(summed, half, axis)
    total = pieces[0]
    for o, piece in zip(order(size)[1:half], pieces[1:]):
        total = total + swap(piece.astype(BF), FC, o).astype(F32)
    return total


def sum_all(x, axis, size):
    step = 1
    while step < size:
        x = x + swap(x, axis, step)
        step *= 2
    return x


def sum_direct(x, axis, size):
    pieces = [x] + [swap(x, axis, s) for s in range(1, size)]
    while len(pieces) > 1:
        pieces = [a + b for a, b in zip(pieces[::2], pieces[1::2])]
    return pieces[0]


def row_block(x, index, rows):
    return lax.dynamic_slice_in_dim(x, index * rows, rows, 0)


def tp_scatter_rows(partial_sum, work=()):
    tp, t = lax.axis_size("tp"), lax.axis_index("tp")
    rows = partial_sum.shape[0] // tp
    arrived = [
        swap(row_block(partial_sum, t ^ s, rows).astype(BF), "tp", s) for s in range(1, tp)
    ]
    arrived, work = lax.optimization_barrier((arrived, work))
    total = row_block(partial_sum, t, rows)
    for piece in arrived:
        total = total + piece.astype(F32)
    return total, work


def put_rows(pieces):
    tp, t = lax.axis_size("tp"), lax.axis_index("tp")
    rows = pieces[0].shape[0]
    out = jnp.zeros((rows * tp, pieces[0].shape[1]), pieces[0].dtype)
    for s, piece in enumerate(pieces):
        out = lax.dynamic_update_slice_in_dim(out, piece, (t ^ s) * rows, 0)
    return out


def tp_gather_rows(x, dtype):
    tp = lax.axis_size("tp")
    pieces = [x] + [swap(x, "tp", s) for s in range(1, tp)]
    return put_rows([piece.astype(dtype) for piece in pieces])


def normalise(x):
    center = x - jnp.mean(x, axis=-1, keepdims=True)
    inverse = lax.rsqrt(jnp.mean(center * center, axis=-1, keepdims=True) + EPSILON)
    return center * inverse, inverse


def normalise_back(grad, gain, xhat, inverse):
    gx = grad * gain
    mean_gx = jnp.mean(gx, axis=-1, keepdims=True)
    mean_gxx = jnp.mean(gx * xhat, axis=-1, keepdims=True)
    return (gx - mean_gx - xhat * mean_gxx) * inverse


def nt(a, b):
    return lax.dot_general(a, b, (((1,), (1,)), ((), ())), preferred_element_type=F32)


def tn(a, b):
    return lax.dot_general(a, b, (((0,), (0,)), ((), ())), preferred_element_type=F32)


def attend_kernel(blocks, *refs):
    q_ref, bias_ref = refs[0], refs[1]
    k_refs, v_refs = refs[2 : 2 + blocks], refs[2 + blocks : 2 + 2 * blocks]
    out_ref, total_ref = refs[2 + 2 * blocks :]
    rows = q_ref.shape[0]
    for h in range(q_ref.shape[1] // HEAD_DIM):
        cols = slice(h * HEAD_DIM, (h + 1) * HEAD_DIM)
        q = q_ref[:, cols]
        scores = [
            nt(k_refs[b][:, cols], q) + bias_ref[b * rows : (b + 1) * rows, :]
            for b in range(blocks)
        ]
        highest = scores[0].max(axis=0, keepdims=True)
        for s in scores[1:]:
            highest = jnp.maximum(highest, s.max(axis=0, keepdims=True))
        weights = [jnp.exp(s - highest) for s in scores]
        summed = sum(w.sum(axis=0, keepdims=True) for w in weights)
        scale = 1.0 / summed
        mixed = sum(
            tn(v_refs[b][:, cols], (weights[b] * scale).astype(BF)) for b in range(blocks)
        )
        out_ref[:, cols] = mixed.T.astype(BF)
        total_ref[0, h : h + 1, :] = highest + jnp.log(summed)


def attend_back_kernel(blocks, *refs):
    q_ref, grad_ref, bias_ref, total_ref = refs[:4]
    kv_refs, outs = refs[4 : 4 + blocks], refs[4 + blocks :]
    gq_ref, gkv_refs = outs[0], outs[1:]
    rows, width = q_ref.shape
    for h in range(q_ref.shape[1] // HEAD_DIM):
        cols = slice(h * HEAD_DIM, (h + 1) * HEAD_DIM)
        q, grad = q_ref[:, cols], grad_ref[:, cols]
        values = slice(width + h * HEAD_DIM, width + (h + 1) * HEAD_DIM)
        total = total_ref[h // 2, h % 2 : h % 2 + 1, :]
        probs, grads = [], []
        for b in range(blocks):
            s = nt(kv_refs[b][:, cols], q) + bias_ref[b * rows : (b + 1) * rows, :]
            probs.append(jnp.exp(s - total))
            grads.append(nt(kv_refs[b][:, values], grad))
        inner = sum((p * g).sum(axis=0, keepdims=True) for p, g in zip(probs, grads))
        gq = None
        for b in range(blocks):
            gs = (probs[b] * (grads[b] - inner)).astype(BF)
            gk = jnp.dot(gs, q, preferred_element_type=F32)
            gv = jnp.dot(probs[b].astype(BF), grad, preferred_element_type=F32)
            low, high = h * HEAD_DIM, (h + 1) * HEAD_DIM
            gkv_refs[b][:, low:high] = gk.astype(gkv_refs[b].dtype)
            gkv_refs[b][:, width + low : width + high] = gv.astype(gkv_refs[b].dtype)
            part = tn(kv_refs[b][:, cols], gs)
            gq = part if gq is None else gq + part
        gq_ref[:, cols] = (gq.T * (1.0 / math.sqrt(HEAD_DIM))).astype(gq_ref.dtype)


def attention_specs(rows, width, blocks):
    pair = 2 * HEAD_DIM
    steps = width // pair
    tile = pl.BlockSpec((rows, pair), lambda j: (0, j))
    value_tile = pl.BlockSpec((rows, pair), lambda j: (0, steps + j))
    bias = pl.BlockSpec((blocks * rows, rows), lambda j: (0, 0))
    total = pl.BlockSpec((1, 2, rows), lambda j: (j, 0, 0))
    return steps, tile, value_tile, bias, total


def attend(q, kv, bias):
    rows, width = q.shape
    blocks = len(kv)
    steps, tile, value_tile, bias_spec, total = attention_specs(rows, width, blocks)
    return pl.pallas_call(
        partial(attend_kernel, blocks),
        grid=(steps,),
        in_specs=[tile, bias_spec] + [tile] * blocks + [value_tile] * blocks,
        out_specs=[tile, total],
        out_shape=[
            jax.ShapeDtypeStruct((rows, width), BF),
            jax.ShapeDtypeStruct((steps, 2, rows), F32),
        ],
        cost_estimate=pl.CostEstimate(
            flops=4 * blocks * rows * rows * width,
            bytes_accessed=4 * blocks * rows * (rows + width),
            transcendentals=blocks * rows * rows * width // HEAD_DIM,
        ),
        name="attend",
    )(q, bias, *kv, *kv)


def attend_back(q, kv, bias, totals, grad):
    rows, width = q.shape
    blocks = len(kv)
    kinds = [F32] + [BF] * (blocks - 1)
    return pl.pallas_call(
        partial(attend_back_kernel, blocks),
        out_shape=[jax.ShapeDtypeStruct((rows, width), BF)]
        + [jax.ShapeDtypeStruct((rows, 2 * width), k) for k in kinds],
        cost_estimate=pl.CostEstimate(
            flops=10 * blocks * rows * rows * width,
            bytes_accessed=4 * blocks * rows * (rows + width),
            transcendentals=blocks * rows * rows * width // HEAD_DIM,
        ),
        name="attend_back",
    )(q, grad, bias, totals, *kv)


def local(
    tokens,
    segment_ids,
    first_gain,
    first_shift,
    input_weight,
    input_bias,
    output_weight,
    output_bias,
    second_gain,
    second_shift,
    up_weight,
    up_bias,
    down_weight,
    down_bias,
    cotangent,
):
    sequences, rows, features = tokens.shape
    ctx, tp = lax.axis_size("ctx"), lax.axis_size("tp")
    c, t = lax.axis_index("ctx"), lax.axis_index("tp")
    size = group_size()
    half = features // 2
    chunk = rows // tp
    width = input_weight.shape[2]
    earlier = min(ctx - 1, -(-(MAX_SEGMENT - 1) // rows))
    blocks = earlier + 1

    vectors = jnp.stack(
        [first_gain, first_shift, output_bias, second_gain, second_shift, down_bias]
    )
    first_shard = jnp.concatenate(
        [
            jnp.swapaxes(input_weight, 1, 2).reshape(3 * width, -1),
            jnp.pad(vectors, ((0, 26), (0, 0))),
        ],
        axis=0,
    )
    first_full, first_even = gather_columns(first_shard)
    in_full = first_full[: 3 * width]
    vectors_full = first_full[3 * width :].astype(F32)
    gain_one, shift_one, out_shift, gain_two, shift_two, down_shift = [
        vectors_full[i : i + 1] for i in range(6)
    ]
    out_rows = jnp.concatenate(
        [output_weight] + [swap(output_weight, "tp", s) for s in range(1, tp)], axis=0
    )
    ff_shard = jnp.concatenate([up_weight.T, down_weight], axis=0)

    resid = to_relative(tokens.reshape(rows, features)).astype(F32)
    cot_low = to_relative(cotangent.reshape(rows, features))
    xhat_one, inverse_one = normalise(resid)
    normed_low = (xhat_one * gain_one + shift_one).astype(BF)

    ids = segment_ids.reshape(-1)
    query_seg = lax.dynamic_slice_in_dim(ids, c * rows, rows, 0)
    padded = jnp.concatenate([jnp.full((earlier * rows,), -1, ids.dtype), ids])
    biases = []
    for b in range(blocks):
        key_seg = lax.dynamic_slice_in_dim(padded, (c + earlier - b) * rows, rows, 0)
        allowed = key_seg[:, None] == query_seg[None, :]
        if b == 0:
            place = jnp.arange(rows)
            allowed = allowed & (place[:, None] <= place[None, :])
        biases.append(jnp.where(allowed, 0.0, -1e30).astype(F32))
    bias = jnp.concatenate(biases, axis=0)

    in_bias = jnp.concatenate([input_bias[0], jnp.zeros_like(input_bias[0]), input_bias[1]])
    projected = (nt(normed_low, in_full) + in_bias.astype(F32)).astype(BF)
    queries = projected[:, :width] * jnp.asarray(1.0 / math.sqrt(HEAD_DIM), BF)
    kv = [projected[:, width:]]
    for b in range(1, blocks):
        kv.append(lax.ppermute(kv[0], "ctx", [(i, i + b) for i in range(ctx - b)]))
    out_full, out_even = gather_columns(gate(out_rows, first_even))
    ff_full, ff_even = gather_columns(gate(ff_shard, (kv[-1], out_even)))
    hidden_width = up_weight.shape[1]
    up_full, down_full = ff_full[:hidden_width], ff_full[hidden_width:]

    mixed, totals = attend(queries, kv, bias)
    mixed_all = jnp.concatenate(
        [mixed] + [swap(mixed, "tp", s) for s in range(1, tp)], axis=1
    )
    middle = resid + out_shift + jnp.dot(mixed_all, out_full, preferred_element_type=F32)
    xhat_two, inverse_two = normalise(middle)
    normed_two = (xhat_two * gain_two + shift_two).astype(BF)
    hidden = nt(normed_two, up_full) + up_bias.astype(F32)
    gelu_tanh = partial(jax.nn.gelu, approximate=True)
    active, gelu_pullback = jax.vjp(gelu_tanh, hidden)
    active = active.astype(BF)
    grad_active = jnp.dot(cot_low, down_full.T, preferred_element_type=F32)
    grad_hidden = gelu_pullback(grad_active)[0].astype(BF)
    grad_norm_two, ff_grads = tp_scatter_rows(
        jnp.dot(grad_hidden, up_full, preferred_element_type=F32),
        (
            tn(normed_two[:, half:], grad_hidden).astype(BF),
            tn(active, cot_low[:, half:]).astype(BF),
            tn(normed_two[:, :half], grad_hidden),
            tn(active, cot_low[:, :half]),
        ),
    )
    up_grad = scatter_sum(ff_grads[2], ff_grads[0], 0)
    down_grad = scatter_sum(ff_grads[3], ff_grads[1], 1)
    grad_up_bias = jnp.sum(grad_hidden.astype(F32), axis=0)

    middle_rows = row_block(middle, t, chunk)
    xhat_rows, inverse_rows = row_block(xhat_two, t, chunk), row_block(inverse_two, t, chunk)
    cot_rows = row_block(cot_low, t, chunk).astype(F32)
    grad_middle = cot_rows + normalise_back(grad_norm_two, gain_two, xhat_rows, inverse_rows)
    grad_attn = grad_middle.astype(BF)
    grad_mixed = nt(grad_attn, out_full).astype(BF)
    grad_pieces = jnp.split(grad_mixed, tp, axis=1)
    mixed_rows = row_block(mixed_all, t, chunk)
    arrived, out_parts = lax.optimization_barrier(
        (
            [swap(grad_pieces[s], "tp", s) for s in range(1, tp)],
            (
                tn(mixed_rows, grad_attn[:, :half]),
                tn(mixed_rows, grad_attn[:, half:]).astype(BF),
            ),
        )
    )
    grad_heads = put_rows([grad_pieces[0]] + arrived)

    late_active = gate(active, grad_heads)
    mlp_part = jnp.dot(late_active, down_full, preferred_element_type=F32)
    result_rows = middle_rows + tp_scatter_rows(mlp_part)[0] + down_shift
    result = tp_gather_rows(to_absolute(result_rows.astype(BF)), BF)

    grads = attend_back(queries, kv, bias, totals, grad_heads)
    grad_queries = grads[0]
    grad_kv = grads[1]
    for b in range(1, blocks):
        back = [(i + b, i) for i in range(ctx - b)]
        grad_kv = grad_kv + lax.ppermute(grads[1 + b], "ctx", back).astype(F32)
    grad_joined = jnp.concatenate([grad_queries, grad_kv.astype(BF)], axis=1)
    out_grad = scatter_sum(out_parts[0], out_parts[1], 1)
    out_blocks = jnp.split(out_grad, tp, axis=0)
    out_weight_grad = out_blocks[0]
    for s in range(1, tp):
        out_weight_grad = out_weight_grad + swap(out_blocks[s].astype(BF), "tp", s).astype(F32)

    grad_norm_one, in_parts = tp_scatter_rows(
        jnp.dot(grad_joined, in_full, preferred_element_type=F32),
        (tn(normed_low[:, half:], grad_joined).astype(BF), tn(normed_low[:, :half], grad_joined)),
    )
    in_grad = scatter_sum(in_parts[1], in_parts[0], 0)
    in_weight_grad = jnp.stack([in_grad[:, i * width : (i + 1) * width] for i in range(3)])
    grad_in_bias = jnp.sum(grad_joined.astype(F32), axis=0)
    grad_in_bias = jnp.concatenate([grad_in_bias[:width], grad_in_bias[2 * width :]])
    bias_sums = sum_all(jnp.concatenate([grad_in_bias, grad_up_bias])[None, :], FC, size)[0]

    xhat_one_rows = row_block(xhat_one, t, chunk)
    inverse_one_rows = row_block(inverse_one, t, chunk)
    tokens_grad_rows = grad_middle + normalise_back(
        grad_norm_one, gain_one, xhat_one_rows, inverse_one_rows
    )
    tokens_grad = tp_gather_rows(to_absolute(tokens_grad_rows.astype(BF)), F32)

    sums = jnp.stack(
        [
            jnp.sum(grad_norm_one * xhat_one_rows, axis=0),
            jnp.sum(grad_norm_one, axis=0),
            jnp.sum(grad_attn.astype(F32), axis=0),
            jnp.sum(grad_norm_two * xhat_rows, axis=0),
            jnp.sum(grad_norm_two, axis=0),
            jnp.sum(cot_rows, axis=0),
        ]
    )
    sums = sum_direct(sums, "tp", tp)
    vector_grads = scatter_sum(sums[:, :half], sums[:, half:], 1)
    return (
        result.reshape(sequences, rows, features),
        tokens_grad.reshape(sequences, rows, features),
        vector_grads[0],
        vector_grads[1],
        in_weight_grad,
        bias_sums[: 2 * width].reshape(2, width),
        out_weight_grad,
        vector_grads[2],
        vector_grads[3],
        vector_grads[4],
        up_grad,
        bias_sums[2 * width :],
        down_grad,
        vector_grads[5],
    )


def solution(mesh):
    in_specs = (
        P("fsdp", "ctx", None),
        P("fsdp", None),
        P(("fsdp", "ctx")),
        P(("fsdp", "ctx")),
        P(None, ("fsdp", "ctx"), "tp"),
        P(None, "tp"),
        P("tp", ("fsdp", "ctx")),
        P(("fsdp", "ctx")),
        P(("fsdp", "ctx")),
        P(("fsdp", "ctx")),
        P(("fsdp", "ctx"), "tp"),
        P("tp"),
        P("tp", ("fsdp", "ctx")),
        P(("fsdp", "ctx")),
        P("fsdp", "ctx", None),
    )
    out_specs = (
        P("fsdp", "ctx", None),
        P("fsdp", "ctx", None),
        P(("fsdp", "ctx")),
        P(("fsdp", "ctx")),
        P(None, ("fsdp", "ctx"), "tp"),
        P(None, "tp"),
        P("tp", ("fsdp", "ctx")),
        P(("fsdp", "ctx")),
        P(("fsdp", "ctx")),
        P(("fsdp", "ctx")),
        P(("fsdp", "ctx"), "tp"),
        P("tp"),
        P("tp", ("fsdp", "ctx")),
        P(("fsdp", "ctx")),
    )
    return jax.shard_map(local, mesh=mesh, in_specs=in_specs, out_specs=out_specs, check_vma=False)
```

```python
from functools import partial
import math

import jax
import jax.numpy as jnp
from jax import lax
from jax.experimental import pallas as pl
from jax.sharding import PartitionSpec as P


HEAD_DIM = 64
MAX_SEGMENT = 576
EPSILON = 1e-05
FC = ("fsdp", "ctx")
BF = jnp.bfloat16
F32 = jnp.float32


def swap(x, axis, offset):
    size = lax.axis_size(axis)
    return lax.ppermute(x, axis, [(i, i ^ offset) for i in range(size)])


def order(size):
    return [2 * i for i in range(size // 2)] + [2 * i + 1 for i in range(size // 2)]


def place_of(offset, size):
    return (offset & 1) * (size // 2) + (offset >> 1)


def device_index():
    return lax.axis_index("fsdp") * lax.axis_size("ctx") + lax.axis_index("ctx")


def group_size():
    return lax.axis_size("fsdp") * lax.axis_size("ctx")


def to_relative(x):
    size, me = group_size(), device_index()
    width = x.shape[1] // size
    return jnp.concatenate(
        [lax.dynamic_slice_in_dim(x, (me ^ o) * width, width, 1) for o in order(size)], axis=1
    )


def to_absolute(x):
    size, me = group_size(), device_index()
    width = x.shape[1] // size
    return jnp.concatenate(
        [
            lax.dynamic_slice_in_dim(x, place_of(me ^ j, size) * width, width, 1)
            for j in range(size)
        ],
        axis=1,
    )


def join_kernel(*refs):
    out_ref = refs[-1]
    width = refs[0].shape[1]
    for i, ref in enumerate(refs[:-1]):
        out_ref[:, i * width : (i + 1) * width] = ref[...]


def join(pieces):
    rows, width = pieces[0].shape
    tile = max(d for d in range(16, min(rows, 1024) + 1, 16) if rows % d == 0)
    total = width * len(pieces)
    return pl.pallas_call(
        join_kernel,
        grid=(rows // tile,),
        in_specs=[pl.BlockSpec((tile, width), lambda i: (i, 0))] * len(pieces),
        out_specs=pl.BlockSpec((tile, total), lambda i: (i, 0)),
        out_shape=jax.ShapeDtypeStruct((rows, total), pieces[0].dtype),
        cost_estimate=pl.CostEstimate(
            flops=0, bytes_accessed=4 * rows * total, transcendentals=0
        ),
        name="join",
    )(*pieces)


def gather_columns(w):
    size = group_size()
    if size > 8:
        picked = jnp.take(
            lax.all_gather(w, FC), device_index() ^ jnp.array(order(size)), axis=0
        )
        full = jnp.moveaxis(picked, 0, 1).reshape(w.shape[0], -1)
        return jnp.split(full, 2, axis=1)
    pieces = [w] + [swap(w, FC, o) for o in order(size)[1 : size // 2]]
    even = join(pieces)
    return even, swap(even, FC, 1)


def scatter_sum(even, odd, axis):
    size = group_size()
    half = size // 2
    if size > 8:
        pieces = jnp.stack(jnp.split(even, half, axis) + jnp.split(odd, half, axis)).astype(BF)
        wanted = place_of(device_index() ^ jnp.arange(size), size)
        parts = lax.all_to_all(jnp.take(pieces, wanted, axis=0), FC, 0, 0, tiled=True)
        return jnp.sum(parts.astype(F32), axis=0)
    summed = even.astype(F32) + swap(odd.astype(BF), FC, 1).astype(F32)
    pieces = jnp.split(summed, half, axis)
    total = pieces[0]
    for o, piece in zip(order(size)[1:half], pieces[1:]):
        total = total + swap(piece.astype(BF), FC, o).astype(F32)
    return total


def sum_all(x, axis, size):
    step = 1
    while step < size:
        x = x + swap(x, axis, step)
        step *= 2
    return x


def sum_direct(x, axis, size):
    pieces = [x] + [swap(x, axis, s) for s in range(1, size)]
    while len(pieces) > 1:
        pieces = [a + b for a, b in zip(pieces[::2], pieces[1::2])]
    return pieces[0]


def row_block(x, index, rows):
    return lax.dynamic_slice_in_dim(x, index * rows, rows, 0)


def tp_scatter_rows(halves):
    tp, t = lax.axis_size("tp"), lax.axis_index("tp")
    rows = halves[0].shape[0] // tp
    total = jnp.concatenate([row_block(h, t, rows) for h in halves], axis=1)
    for s in range(1, tp):
        block = [row_block(h, t ^ s, rows).astype(BF) for h in halves]
        block = jnp.concatenate(block, axis=1) if len(block) > 1 else block[0]
        total = total + swap(block, "tp", s).astype(F32)
    return total


def put_rows(pieces):
    tp, t = lax.axis_size("tp"), lax.axis_index("tp")
    rows = pieces[0].shape[0]
    out = jnp.zeros((rows * tp, pieces[0].shape[1]), pieces[0].dtype)
    for s, piece in enumerate(pieces):
        out = lax.dynamic_update_slice_in_dim(out, piece, (t ^ s) * rows, 0)
    return out


def tp_gather_rows(x, dtype):
    tp = lax.axis_size("tp")
    pieces = [x] + [swap(x, "tp", s) for s in range(1, tp)]
    return put_rows([piece.astype(dtype) for piece in pieces])


def normalise(x):
    center = x - jnp.mean(x, axis=-1, keepdims=True)
    inverse = lax.rsqrt(jnp.mean(center * center, axis=-1, keepdims=True) + EPSILON)
    return center * inverse, inverse


def normalise_back(grad, gain, xhat, inverse):
    gx = grad * gain
    mean_gx = jnp.mean(gx, axis=-1, keepdims=True)
    mean_gxx = jnp.mean(gx * xhat, axis=-1, keepdims=True)
    return (gx - mean_gx - xhat * mean_gxx) * inverse


def nt(a, b):
    return lax.dot_general(a, b, (((1,), (1,)), ((), ())), preferred_element_type=F32)


def mm(a, b):
    return jnp.dot(a, b, preferred_element_type=F32)


def tn(a, b):
    return lax.dot_general(a, b, (((0,), (0,)), ((), ())), preferred_element_type=F32)


def attend_kernel(blocks, *refs):
    q_ref, bias_ref = refs[0], refs[1]
    k_refs, v_refs = refs[2 : 2 + blocks], refs[2 + blocks : 2 + 2 * blocks]
    out_ref, total_ref = refs[2 + 2 * blocks :]
    rows = q_ref.shape[0]
    for h in range(q_ref.shape[1] // HEAD_DIM):
        cols = slice(h * HEAD_DIM, (h + 1) * HEAD_DIM)
        q = q_ref[:, cols]
        scores = [
            nt(k_refs[b][:, cols], q) + bias_ref[b * rows : (b + 1) * rows, :]
            for b in range(blocks)
        ]
        highest = scores[0].max(axis=0, keepdims=True)
        for s in scores[1:]:
            highest = jnp.maximum(highest, s.max(axis=0, keepdims=True))
        weights = [jnp.exp(s - highest) for s in scores]
        summed = sum(w.sum(axis=0, keepdims=True) for w in weights)
        scale = 1.0 / summed
        mixed = sum(
            tn(v_refs[b][:, cols], (weights[b] * scale).astype(BF)) for b in range(blocks)
        )
        out_ref[:, cols] = mixed.T.astype(BF)
        total_ref[0, h : h + 1, :] = highest + jnp.log(summed)


def attend_back_kernel(blocks, *refs):
    q_ref, grad_ref, bias_ref, total_ref = refs[:4]
    kv_refs, outs = refs[4 : 4 + blocks], refs[4 + blocks :]
    gq_ref, gkv_refs = outs[0], outs[1:]
    rows, width = q_ref.shape
    for h in range(q_ref.shape[1] // HEAD_DIM):
        cols = slice(h * HEAD_DIM, (h + 1) * HEAD_DIM)
        q, grad = q_ref[:, cols], grad_ref[:, cols]
        values = slice(width + h * HEAD_DIM, width + (h + 1) * HEAD_DIM)
        total = total_ref[h // 2, h % 2 : h % 2 + 1, :]
        probs, grads = [], []
        for b in range(blocks):
            s = nt(kv_refs[b][:, cols], q) + bias_ref[b * rows : (b + 1) * rows, :]
            probs.append(jnp.exp(s - total))
            grads.append(nt(kv_refs[b][:, values], grad))
        inner = sum((p * g).sum(axis=0, keepdims=True) for p, g in zip(probs, grads))
        gq = None
        for b in range(blocks):
            gs = (probs[b] * (grads[b] - inner)).astype(BF)
            gk = jnp.dot(gs, q, preferred_element_type=F32)
            gv = jnp.dot(probs[b].astype(BF), grad, preferred_element_type=F32)
            low, high = h * HEAD_DIM, (h + 1) * HEAD_DIM
            gkv_refs[b][:, low:high] = gk.astype(gkv_refs[b].dtype)
            gkv_refs[b][:, width + low : width + high] = gv.astype(gkv_refs[b].dtype)
            part = tn(kv_refs[b][:, cols], gs)
            gq = part if gq is None else gq + part
        gq_ref[:, cols] = (gq.T * (1.0 / math.sqrt(HEAD_DIM))).astype(gq_ref.dtype)


def attention_specs(rows, width, blocks):
    pair = 2 * HEAD_DIM
    steps = width // pair
    tile = pl.BlockSpec((rows, pair), lambda j: (0, j))
    value_tile = pl.BlockSpec((rows, pair), lambda j: (0, steps + j))
    bias = pl.BlockSpec((blocks * rows, rows), lambda j: (0, 0))
    total = pl.BlockSpec((1, 2, rows), lambda j: (j, 0, 0))
    return steps, tile, value_tile, bias, total


def attend(q, kv, bias):
    rows, width = q.shape
    blocks = len(kv)
    steps, tile, value_tile, bias_spec, total = attention_specs(rows, width, blocks)
    return pl.pallas_call(
        partial(attend_kernel, blocks),
        grid=(steps,),
        in_specs=[tile, bias_spec] + [tile] * blocks + [value_tile] * blocks,
        out_specs=[tile, total],
        out_shape=[
            jax.ShapeDtypeStruct((rows, width), BF),
            jax.ShapeDtypeStruct((steps, 2, rows), F32),
        ],
        cost_estimate=pl.CostEstimate(
            flops=4 * blocks * rows * rows * width,
            bytes_accessed=4 * blocks * rows * (rows + width),
            transcendentals=blocks * rows * rows * width // HEAD_DIM,
        ),
        name="attend",
    )(q, bias, *kv, *kv)


def attend_back(q, kv, bias, totals, grad):
    rows, width = q.shape
    blocks = len(kv)
    kinds = [F32] + [BF] * (blocks - 1)
    return pl.pallas_call(
        partial(attend_back_kernel, blocks),
        out_shape=[jax.ShapeDtypeStruct((rows, width), BF)]
        + [jax.ShapeDtypeStruct((rows, 2 * width), k) for k in kinds],
        cost_estimate=pl.CostEstimate(
            flops=10 * blocks * rows * rows * width,
            bytes_accessed=4 * blocks * rows * (rows + width),
            transcendentals=blocks * rows * rows * width // HEAD_DIM,
        ),
        name="attend_back",
    )(q, grad, bias, totals, *kv)


def local(
    tokens,
    segment_ids,
    first_gain,
    first_shift,
    input_weight,
    input_bias,
    output_weight,
    output_bias,
    second_gain,
    second_shift,
    up_weight,
    up_bias,
    down_weight,
    down_bias,
    cotangent,
):
    sequences, rows, features = tokens.shape
    ctx, tp = lax.axis_size("ctx"), lax.axis_size("tp")
    c, t = lax.axis_index("ctx"), lax.axis_index("tp")
    size = group_size()
    half = features // 2
    chunk = rows // tp
    width = input_weight.shape[2]
    earlier = min(ctx - 1, -(-(MAX_SEGMENT - 1) // rows))
    blocks = earlier + 1

    vectors = jnp.stack(
        [first_gain, first_shift, output_bias, second_gain, second_shift, down_bias]
    )
    first_shard = jnp.concatenate(
        [
            jnp.swapaxes(input_weight, 1, 2).reshape(3 * width, -1),
            jnp.pad(vectors, ((0, 26), (0, 0))),
        ],
        axis=0,
    )
    first_full = join(list(gather_columns(first_shard)))
    in_full = first_full[: 3 * width]
    vectors_full = first_full[3 * width :].astype(F32)
    gain_one, shift_one, out_shift, gain_two, shift_two, down_shift = [
        vectors_full[i : i + 1] for i in range(6)
    ]
    out_rows = jnp.concatenate(
        [output_weight] + [swap(output_weight, "tp", s) for s in range(1, tp)], axis=0
    )
    ff_shard = jnp.concatenate([up_weight.T, down_weight], axis=0)

    resid = to_relative(tokens.reshape(rows, features)).astype(F32)
    cot_low = to_relative(cotangent.reshape(rows, features))
    xhat_one, inverse_one = normalise(resid)
    normed_low = (xhat_one * gain_one + shift_one).astype(BF)

    ids = segment_ids.reshape(-1)
    query_seg = lax.dynamic_slice_in_dim(ids, c * rows, rows, 0)
    padded = jnp.concatenate([jnp.full((earlier * rows,), -1, ids.dtype), ids])
    biases = []
    for b in range(blocks):
        key_seg = lax.dynamic_slice_in_dim(padded, (c + earlier - b) * rows, rows, 0)
        allowed = key_seg[:, None] == query_seg[None, :]
        if b == 0:
            place = jnp.arange(rows)
            allowed = allowed & (place[:, None] <= place[None, :])
        biases.append(jnp.where(allowed, 0.0, -1e30).astype(F32))
    bias = jnp.concatenate(biases, axis=0)

    in_bias = jnp.concatenate([input_bias[0], jnp.zeros_like(input_bias[0]), input_bias[1]])
    projected = (nt(normed_low, in_full) + in_bias.astype(F32)).astype(BF)
    queries = projected[:, :width] * jnp.asarray(1.0 / math.sqrt(HEAD_DIM), BF)
    kv = [projected[:, width:]]
    for b in range(1, blocks):
        kv.append(lax.ppermute(kv[0], "ctx", [(i, i + b) for i in range(ctx - b)]))
    out_full = join(list(gather_columns(out_rows)))
    ff_halves = gather_columns(ff_shard)
    hidden_width = up_weight.shape[1]
    up_even, up_odd = [w[:hidden_width] for w in ff_halves]
    down_even, down_odd = [w[hidden_width:] for w in ff_halves]

    mixed, totals = attend(queries, kv, bias)
    mixed_all = jnp.concatenate([mixed] + [swap(mixed, "tp", s) for s in range(1, tp)], axis=1)
    middle = resid + out_shift + jnp.dot(mixed_all, out_full, preferred_element_type=F32)
    xhat_two, inverse_two = normalise(middle)
    normed_two = (xhat_two * gain_two + shift_two).astype(BF)
    hidden = nt(normed_two[:, :half], up_even) + nt(normed_two[:, half:], up_odd)
    hidden = hidden + up_bias.astype(F32)
    gelu_tanh = partial(jax.nn.gelu, approximate=True)
    active, gelu_pullback = jax.vjp(gelu_tanh, hidden)
    active = active.astype(BF)
    grad_active = nt(cot_low[:, :half], down_even) + nt(cot_low[:, half:], down_odd)
    grad_hidden = gelu_pullback(grad_active)[0].astype(BF)
    grad_norm_two = tp_scatter_rows([mm(grad_hidden, up_even), mm(grad_hidden, up_odd)])
    up_grad = scatter_sum(
        tn(normed_two[:, :half], grad_hidden), tn(normed_two[:, half:], grad_hidden), 0
    )
    down_grad = scatter_sum(tn(active, cot_low[:, :half]), tn(active, cot_low[:, half:]), 1)
    grad_up_bias = jnp.sum(grad_hidden.astype(F32), axis=0)

    middle_rows = row_block(middle, t, chunk)
    xhat_rows, inverse_rows = row_block(xhat_two, t, chunk), row_block(inverse_two, t, chunk)
    cot_rows = row_block(cot_low, t, chunk).astype(F32)
    grad_middle = cot_rows + normalise_back(grad_norm_two, gain_two, xhat_rows, inverse_rows)
    grad_attn = grad_middle.astype(BF)
    grad_mixed = nt(grad_attn, out_full).astype(BF)
    grad_pieces = jnp.split(grad_mixed, tp, axis=1)
    mixed_rows = row_block(mixed_all, t, chunk)
    grad_heads = put_rows([grad_pieces[0]] + [swap(grad_pieces[s], "tp", s) for s in range(1, tp)])

    mlp_halves = [mm(active, down_even), mm(active, down_odd)]
    result_rows = middle_rows + tp_scatter_rows(mlp_halves) + down_shift
    result = tp_gather_rows(to_absolute(result_rows.astype(BF)), BF)

    grads = attend_back(queries, kv, bias, totals, grad_heads)
    grad_queries = grads[0]
    grad_kv = grads[1]
    for b in range(1, blocks):
        back = [(i + b, i) for i in range(ctx - b)]
        arrived = lax.ppermute(grads[1 + b], "ctx", back)
        grad_kv = grad_kv + arrived.astype(F32)
    grad_joined = jnp.concatenate([grad_queries, grad_kv.astype(BF)], axis=1)
    out_grad = scatter_sum(
        tn(mixed_rows, grad_attn[:, :half]), tn(mixed_rows, grad_attn[:, half:]), 1
    )
    out_blocks = jnp.split(out_grad, tp, axis=0)
    out_weight_grad = out_blocks[0]
    for s in range(1, tp):
        out_weight_grad = out_weight_grad + swap(out_blocks[s].astype(BF), "tp", s).astype(F32)

    grad_norm_one = tp_scatter_rows([mm(grad_joined, in_full)])
    in_grad = scatter_sum(
        tn(normed_low[:, :half], grad_joined), tn(normed_low[:, half:], grad_joined), 0
    )
    in_weight_grad = jnp.stack([in_grad[:, i * width : (i + 1) * width] for i in range(3)])
    grad_in_bias = jnp.sum(grad_joined.astype(F32), axis=0)
    grad_in_bias = jnp.concatenate([grad_in_bias[:width], grad_in_bias[2 * width :]])
    bias_sums = sum_all(jnp.concatenate([grad_in_bias, grad_up_bias])[None, :], FC, size)[0]

    xhat_one_rows = row_block(xhat_one, t, chunk)
    inverse_one_rows = row_block(inverse_one, t, chunk)
    tokens_grad_rows = grad_middle + normalise_back(
        grad_norm_one, gain_one, xhat_one_rows, inverse_one_rows
    )
    tokens_grad = tp_gather_rows(to_absolute(tokens_grad_rows.astype(BF)), F32)

    sums = jnp.stack(
        [
            jnp.sum(grad_norm_one * xhat_one_rows, axis=0),
            jnp.sum(grad_norm_one, axis=0),
            jnp.sum(grad_attn.astype(F32), axis=0),
            jnp.sum(grad_norm_two * xhat_rows, axis=0),
            jnp.sum(grad_norm_two, axis=0),
            jnp.sum(cot_rows, axis=0),
        ]
    )
    sums = sum_direct(sums, "tp", tp)
    vector_grads = scatter_sum(sums[:, :half], sums[:, half:], 1)
    return (
        result.reshape(sequences, rows, features),
        tokens_grad.reshape(sequences, rows, features),
        vector_grads[0],
        vector_grads[1],
        in_weight_grad,
        bias_sums[: 2 * width].reshape(2, width),
        out_weight_grad,
        vector_grads[2],
        vector_grads[3],
        vector_grads[4],
        up_grad,
        bias_sums[2 * width :],
        down_grad,
        vector_grads[5],
    )


def solution(mesh):
    in_specs = (
        P("fsdp", "ctx", None),
        P("fsdp", None),
        P(("fsdp", "ctx")),
        P(("fsdp", "ctx")),
        P(None, ("fsdp", "ctx"), "tp"),
        P(None, "tp"),
        P("tp", ("fsdp", "ctx")),
        P(("fsdp", "ctx")),
        P(("fsdp", "ctx")),
        P(("fsdp", "ctx")),
        P(("fsdp", "ctx"), "tp"),
        P("tp"),
        P("tp", ("fsdp", "ctx")),
        P(("fsdp", "ctx")),
        P("fsdp", "ctx", None),
    )
    out_specs = (
        P("fsdp", "ctx", None),
        P("fsdp", "ctx", None),
        P(("fsdp", "ctx")),
        P(("fsdp", "ctx")),
        P(None, ("fsdp", "ctx"), "tp"),
        P(None, "tp"),
        P("tp", ("fsdp", "ctx")),
        P(("fsdp", "ctx")),
        P(("fsdp", "ctx")),
        P(("fsdp", "ctx")),
        P(("fsdp", "ctx"), "tp"),
        P("tp"),
        P("tp", ("fsdp", "ctx")),
        P(("fsdp", "ctx")),
    )
    return jax.shard_map(
        local,
        mesh=mesh,
        in_specs=in_specs,
        out_specs=out_specs,
        check_vma=False,
    )
```

```python
from functools import partial
import math

import jax
import jax.numpy as jnp
from jax import lax
from jax.experimental import pallas as pl
from jax.sharding import PartitionSpec as P


HEAD_DIM = 64
MAX_SEGMENT = 576
EPSILON = 1e-05
FC = ("fsdp", "ctx")
BF = jnp.bfloat16
F32 = jnp.float32


def swap(x, axis, offset):
    size = lax.axis_size(axis)
    return lax.ppermute(x, axis, [(i, i ^ offset) for i in range(size)])


def order(size):
    return [2 * i for i in range(size // 2)] + [2 * i + 1 for i in range(size // 2)]


def place_of(offset, size):
    return (offset & 1) * (size // 2) + (offset >> 1)


def device_index():
    return lax.axis_index("fsdp") * lax.axis_size("ctx") + lax.axis_index("ctx")


def group_size():
    return lax.axis_size("fsdp") * lax.axis_size("ctx")


def to_relative(x):
    size, me = group_size(), device_index()
    width = x.shape[1] // size
    return jnp.concatenate(
        [lax.dynamic_slice_in_dim(x, (me ^ o) * width, width, 1) for o in order(size)], axis=1
    )


def to_absolute(x):
    size, me = group_size(), device_index()
    width = x.shape[1] // size
    return jnp.concatenate(
        [
            lax.dynamic_slice_in_dim(x, place_of(me ^ j, size) * width, width, 1)
            for j in range(size)
        ],
        axis=1,
    )


def join_kernel(*refs):
    out_ref = refs[-1]
    width = refs[0].shape[1]
    for i, ref in enumerate(refs[:-1]):
        out_ref[:, i * width : (i + 1) * width] = ref[...]


def join(pieces):
    rows, width = pieces[0].shape
    tile = max(d for d in range(16, min(rows, 1024) + 1, 16) if rows % d == 0)
    total = width * len(pieces)
    return pl.pallas_call(
        join_kernel,
        grid=(rows // tile,),
        in_specs=[pl.BlockSpec((tile, width), lambda i: (i, 0))] * len(pieces),
        out_specs=pl.BlockSpec((tile, total), lambda i: (i, 0)),
        out_shape=jax.ShapeDtypeStruct((rows, total), pieces[0].dtype),
        cost_estimate=pl.CostEstimate(
            flops=0, bytes_accessed=4 * rows * total, transcendentals=0
        ),
        name="join",
    )(*pieces)


def gather_columns(w):
    size = group_size()
    if size > 8:
        picked = jnp.take(
            lax.all_gather(w, FC), device_index() ^ jnp.array(order(size)), axis=0
        )
        full = jnp.moveaxis(picked, 0, 1).reshape(w.shape[0], -1)
        return jnp.split(full, 2, axis=1)
    pieces = [w] + [swap(w, FC, o) for o in order(size)[1 : size // 2]]
    even = join(pieces)
    return even, swap(even, FC, 1)


def scatter_sum(even, odd, axis):
    size = group_size()
    half = size // 2
    if size > 8:
        pieces = jnp.stack(jnp.split(even, half, axis) + jnp.split(odd, half, axis)).astype(BF)
        wanted = place_of(device_index() ^ jnp.arange(size), size)
        parts = lax.all_to_all(jnp.take(pieces, wanted, axis=0), FC, 0, 0, tiled=True)
        return jnp.sum(parts.astype(F32), axis=0)
    arrived = swap(odd.astype(BF), FC, 1)
    summed = even.astype(F32) + arrived.astype(F32)
    pieces = jnp.split(summed, half, axis)
    total = pieces[0]
    for o, piece in zip(order(size)[1:half], pieces[1:]):
        total = total + swap(piece.astype(BF), FC, o).astype(F32)
    return total


def sum_all(x, axis, size):
    step = 1
    while step < size:
        x = x + swap(x, axis, step)
        step *= 2
    return x


def sum_direct(x, axis, size):
    pieces = [x] + [swap(x, axis, s) for s in range(1, size)]
    while len(pieces) > 1:
        pieces = [a + b for a, b in zip(pieces[::2], pieces[1::2])]
    return pieces[0]


def row_block(x, index, rows):
    return lax.dynamic_slice_in_dim(x, index * rows, rows, 0)


def tp_scatter_rows(halves):
    tp, t = lax.axis_size("tp"), lax.axis_index("tp")
    rows = halves[0].shape[0] // tp
    total = jnp.concatenate([row_block(h, t, rows) for h in halves], axis=1)
    for s in range(1, tp):
        block = [row_block(h, t ^ s, rows).astype(BF) for h in halves]
        block = jnp.concatenate(block, axis=1) if len(block) > 1 else block[0]
        total = total + swap(block, "tp", s).astype(F32)
    return total


def put_rows(pieces):
    tp, t = lax.axis_size("tp"), lax.axis_index("tp")
    rows = pieces[0].shape[0]
    out = jnp.zeros((rows * tp, pieces[0].shape[1]), pieces[0].dtype)
    for s, piece in enumerate(pieces):
        out = lax.dynamic_update_slice_in_dim(out, piece, (t ^ s) * rows, 0)
    return out


def tp_gather_rows(x, dtype):
    tp = lax.axis_size("tp")
    pieces = [x] + [swap(x, "tp", s) for s in range(1, tp)]
    return put_rows([piece.astype(dtype) for piece in pieces])


def normalise(x):
    center = x - jnp.mean(x, axis=-1, keepdims=True)
    inverse = lax.rsqrt(jnp.mean(center * center, axis=-1, keepdims=True) + EPSILON)
    return center * inverse, inverse


def normalise_back(grad, gain, xhat, inverse):
    gx = grad * gain
    mean_gx = jnp.mean(gx, axis=-1, keepdims=True)
    mean_gxx = jnp.mean(gx * xhat, axis=-1, keepdims=True)
    return (gx - mean_gx - xhat * mean_gxx) * inverse


def nt(a, b):
    return lax.dot_general(a, b, (((1,), (1,)), ((), ())), preferred_element_type=F32)


def mm(a, b):
    return jnp.dot(a, b, preferred_element_type=F32)


def tn(a, b):
    return lax.dot_general(a, b, (((0,), (0,)), ((), ())), preferred_element_type=F32)


def attend_kernel(blocks, *refs):
    q_ref, bias_ref = refs[0], refs[1]
    k_refs, v_refs = refs[2 : 2 + blocks], refs[2 + blocks : 2 + 2 * blocks]
    out_ref, total_ref = refs[2 + 2 * blocks :]
    rows = q_ref.shape[0]
    for h in range(q_ref.shape[1] // HEAD_DIM):
        cols = slice(h * HEAD_DIM, (h + 1) * HEAD_DIM)
        q = q_ref[:, cols]
        scores = [
            nt(k_refs[b][:, cols], q) + bias_ref[b * rows : (b + 1) * rows, :]
            for b in range(blocks)
        ]
        highest = scores[0].max(axis=0, keepdims=True)
        for s in scores[1:]:
            highest = jnp.maximum(highest, s.max(axis=0, keepdims=True))
        weights = [jnp.exp(s - highest) for s in scores]
        summed = sum(w.sum(axis=0, keepdims=True) for w in weights)
        scale = 1.0 / summed
        mixed = sum(
            tn(v_refs[b][:, cols], (weights[b] * scale).astype(BF)) for b in range(blocks)
        )
        out_ref[:, cols] = mixed.T.astype(BF)
        total_ref[0, h : h + 1, :] = highest + jnp.log(summed)


def attend_back_kernel(blocks, *refs):
    q_ref, grad_ref, bias_ref, total_ref = refs[:4]
    kv_refs, outs = refs[4 : 4 + blocks], refs[4 + blocks :]
    gq_ref, gkv_refs = outs[0], outs[1:]
    rows, width = q_ref.shape
    for h in range(q_ref.shape[1] // HEAD_DIM):
        cols = slice(h * HEAD_DIM, (h + 1) * HEAD_DIM)
        q, grad = q_ref[:, cols], grad_ref[:, cols]
        values = slice(width + h * HEAD_DIM, width + (h + 1) * HEAD_DIM)
        total = total_ref[h // 2, h % 2 : h % 2 + 1, :]
        probs, grads = [], []
        for b in range(blocks):
            s = nt(kv_refs[b][:, cols], q) + bias_ref[b * rows : (b + 1) * rows, :]
            probs.append(jnp.exp(s - total))
            grads.append(nt(kv_refs[b][:, values], grad))
        inner = sum((p * g).sum(axis=0, keepdims=True) for p, g in zip(probs, grads))
        gq = None
        for b in range(blocks):
            gs = (probs[b] * (grads[b] - inner)).astype(BF)
            gk = jnp.dot(gs, q, preferred_element_type=F32)
            gv = jnp.dot(probs[b].astype(BF), grad, preferred_element_type=F32)
            low, high = h * HEAD_DIM, (h + 1) * HEAD_DIM
            gkv_refs[b][:, low:high] = gk.astype(gkv_refs[b].dtype)
            gkv_refs[b][:, width + low : width + high] = gv.astype(gkv_refs[b].dtype)
            part = tn(kv_refs[b][:, cols], gs)
            gq = part if gq is None else gq + part
        gq_ref[:, cols] = (gq.T * (1.0 / math.sqrt(HEAD_DIM))).astype(gq_ref.dtype)


def attention_specs(rows, width, blocks):
    pair = 2 * HEAD_DIM
    steps = width // pair
    tile = pl.BlockSpec((rows, pair), lambda j: (0, j))
    value_tile = pl.BlockSpec((rows, pair), lambda j: (0, steps + j))
    bias = pl.BlockSpec((blocks * rows, rows), lambda j: (0, 0))
    total = pl.BlockSpec((1, 2, rows), lambda j: (j, 0, 0))
    return steps, tile, value_tile, bias, total


def attend(q, kv, bias):
    rows, width = q.shape
    blocks = len(kv)
    steps, tile, value_tile, bias_spec, total = attention_specs(rows, width, blocks)
    return pl.pallas_call(
        partial(attend_kernel, blocks),
        grid=(steps,),
        in_specs=[tile, bias_spec] + [tile] * blocks + [value_tile] * blocks,
        out_specs=[tile, total],
        out_shape=[
            jax.ShapeDtypeStruct((rows, width), BF),
            jax.ShapeDtypeStruct((steps, 2, rows), F32),
        ],
        cost_estimate=pl.CostEstimate(
            flops=4 * blocks * rows * rows * width,
            bytes_accessed=4 * blocks * rows * (rows + width),
            transcendentals=blocks * rows * rows * width // HEAD_DIM,
        ),
        name="attend",
    )(q, bias, *kv, *kv)


def attend_back(q, kv, bias, totals, grad):
    rows, width = q.shape
    blocks = len(kv)
    kinds = [F32] + [BF] * (blocks - 1)
    return pl.pallas_call(
        partial(attend_back_kernel, blocks),
        out_shape=[jax.ShapeDtypeStruct((rows, width), BF)]
        + [jax.ShapeDtypeStruct((rows, 2 * width), k) for k in kinds],
        cost_estimate=pl.CostEstimate(
            flops=10 * blocks * rows * rows * width,
            bytes_accessed=4 * blocks * rows * (rows + width),
            transcendentals=blocks * rows * rows * width // HEAD_DIM,
        ),
        name="attend_back",
    )(q, grad, bias, totals, *kv)


def project_kernel(*refs):
    mixed = jnp.concatenate([ref[...] for ref in refs[:-5]], axis=1)
    even_ref, odd_ref, resid_ref, shift_ref, out_ref = refs[-5:]
    half = even_ref.shape[1]
    for i, weight_ref in enumerate((even_ref, odd_ref)):
        cols = slice(i * half, (i + 1) * half)
        out_ref[:, cols] = resid_ref[:, cols] + shift_ref[:, cols] + mm(mixed, weight_ref[...])


def project(mixed_pieces, halves, resid, shift):
    rows, features = resid.shape
    inner = halves[0].shape[0]
    return pl.pallas_call(
        project_kernel,
        out_shape=jax.ShapeDtypeStruct((rows, features), F32),
        cost_estimate=pl.CostEstimate(
            flops=2 * rows * inner * features,
            bytes_accessed=2 * inner * (rows + features) + 8 * rows * features,
            transcendentals=0,
        ),
        name="project",
    )(*mixed_pieces, *halves, resid, shift)


def local(
    tokens,
    segment_ids,
    first_gain,
    first_shift,
    input_weight,
    input_bias,
    output_weight,
    output_bias,
    second_gain,
    second_shift,
    up_weight,
    up_bias,
    down_weight,
    down_bias,
    cotangent,
):
    sequences, rows, features = tokens.shape
    ctx, tp = lax.axis_size("ctx"), lax.axis_size("tp")
    c, t = lax.axis_index("ctx"), lax.axis_index("tp")
    size = group_size()
    half = features // 2
    chunk = rows // tp
    width = input_weight.shape[2]
    earlier = min(ctx - 1, -(-(MAX_SEGMENT - 1) // rows))
    blocks = earlier + 1

    vectors = jnp.stack(
        [first_gain, first_shift, output_bias, second_gain, second_shift, down_bias]
    )
    first_shard = jnp.concatenate(
        [
            jnp.swapaxes(input_weight, 1, 2).reshape(3 * width, -1),
            jnp.pad(vectors, ((0, 26), (0, 0))),
        ],
        axis=0,
    )
    first_full = join(list(gather_columns(first_shard)))
    in_full = first_full[: 3 * width]
    vectors_full = first_full[3 * width :].astype(F32)
    gain_one, shift_one, out_shift, gain_two, shift_two, down_shift = [
        vectors_full[i : i + 1] for i in range(6)
    ]
    out_rows = jnp.concatenate(
        [output_weight] + [swap(output_weight, "tp", s) for s in range(1, tp)], axis=0
    )
    ff_shard = jnp.concatenate([up_weight.T, down_weight], axis=0)

    resid = to_relative(tokens.reshape(rows, features)).astype(F32)
    cot_low = to_relative(cotangent.reshape(rows, features))
    xhat_one, inverse_one = normalise(resid)
    normed_low = (xhat_one * gain_one + shift_one).astype(BF)

    ids = segment_ids.reshape(-1)
    query_seg = lax.dynamic_slice_in_dim(ids, c * rows, rows, 0)
    padded = jnp.concatenate([jnp.full((earlier * rows,), -1, ids.dtype), ids])
    biases = []
    for b in range(blocks):
        key_seg = lax.dynamic_slice_in_dim(padded, (c + earlier - b) * rows, rows, 0)
        allowed = key_seg[:, None] == query_seg[None, :]
        if b == 0:
            place = jnp.arange(rows)
            allowed = allowed & (place[:, None] <= place[None, :])
        biases.append(jnp.where(allowed, 0.0, -1e30).astype(F32))
    bias = jnp.concatenate(biases, axis=0)

    in_bias = jnp.concatenate([input_bias[0], jnp.zeros_like(input_bias[0]), input_bias[1]])
    projected = (nt(normed_low, in_full) + in_bias.astype(F32)).astype(BF)
    queries = projected[:, :width] * jnp.asarray(1.0 / math.sqrt(HEAD_DIM), BF)
    kv = [projected[:, width:]]
    for b in range(1, blocks):
        kv.append(lax.ppermute(kv[0], "ctx", [(i, i + b) for i in range(ctx - b)]))
    out_halves = gather_columns(out_rows)
    ff_halves = gather_columns(ff_shard)
    hidden_width = up_weight.shape[1]
    up_even, up_odd = [w[:hidden_width] for w in ff_halves]
    down_even, down_odd = [w[hidden_width:] for w in ff_halves]

    mixed, totals = attend(queries, kv, bias)
    mixed_pieces = [mixed] + [swap(mixed, "tp", s) for s in range(1, tp)]
    middle = project(mixed_pieces, out_halves, resid, out_shift)
    xhat_two, inverse_two = normalise(middle)
    normed_two = (xhat_two * gain_two + shift_two).astype(BF)
    hidden = nt(normed_two[:, :half], up_even) + nt(normed_two[:, half:], up_odd)
    hidden = hidden + up_bias.astype(F32)
    gelu_tanh = partial(jax.nn.gelu, approximate=True)
    active, gelu_pullback = jax.vjp(gelu_tanh, hidden)
    active = active.astype(BF)
    grad_active = nt(cot_low[:, :half], down_even) + nt(cot_low[:, half:], down_odd)
    grad_hidden = gelu_pullback(grad_active)[0].astype(BF)
    grad_norm_two = tp_scatter_rows([mm(grad_hidden, up_even), mm(grad_hidden, up_odd)])
    up_parts = tn(normed_two[:, :half], grad_hidden), tn(normed_two[:, half:], grad_hidden)
    down_parts = tn(active, cot_low[:, :half]), tn(active, cot_low[:, half:])
    up_grad = scatter_sum(*up_parts, 0)
    down_grad = scatter_sum(*down_parts, 1)
    grad_up_bias = jnp.sum(grad_hidden.astype(F32), axis=0)

    middle_rows = row_block(middle, t, chunk)
    xhat_rows, inverse_rows = row_block(xhat_two, t, chunk), row_block(inverse_two, t, chunk)
    cot_rows = row_block(cot_low, t, chunk).astype(F32)
    grad_middle = cot_rows + normalise_back(grad_norm_two, gain_two, xhat_rows, inverse_rows)
    grad_attn = grad_middle.astype(BF)
    grad_mixed = nt(grad_attn[:, :half], out_halves[0]) + nt(grad_attn[:, half:], out_halves[1])
    grad_mixed = grad_mixed.astype(BF)
    grad_pieces = jnp.split(grad_mixed, tp, axis=1)
    mixed_rows = jnp.concatenate([row_block(m, t, chunk) for m in mixed_pieces], axis=1)
    grad_heads = put_rows([grad_pieces[0]] + [swap(grad_pieces[s], "tp", s) for s in range(1, tp)])

    mlp_halves = [mm(active, down_even), mm(active, down_odd)]
    result_rows = middle_rows + tp_scatter_rows(mlp_halves) + down_shift
    result = tp_gather_rows(to_absolute(result_rows.astype(BF)), BF)

    grads = attend_back(queries, kv, bias, totals, grad_heads)
    grad_queries = grads[0]
    grad_kv = grads[1]
    for b in range(1, blocks):
        back = [(i + b, i) for i in range(ctx - b)]
        arrived = lax.ppermute(grads[1 + b], "ctx", back)
        grad_kv = grad_kv + arrived.astype(F32)
    grad_joined = jnp.concatenate([grad_queries, grad_kv.astype(BF)], axis=1)
    out_grad = scatter_sum(
        tn(mixed_rows, grad_attn[:, :half]), tn(mixed_rows, grad_attn[:, half:]), 1
    )
    out_blocks = jnp.split(out_grad, tp, axis=0)
    out_weight_grad = out_blocks[0]
    for s in range(1, tp):
        out_weight_grad = out_weight_grad + swap(out_blocks[s].astype(BF), "tp", s).astype(F32)

    grad_norm_one = tp_scatter_rows([mm(grad_joined, in_full)])
    in_parts = tn(normed_low[:, :half], grad_joined), tn(normed_low[:, half:], grad_joined)
    in_grad = scatter_sum(*in_parts, 0)
    in_weight_grad = jnp.stack([in_grad[:, i * width : (i + 1) * width] for i in range(3)])
    grad_in_bias = jnp.sum(grad_joined.astype(F32), axis=0)
    grad_in_bias = jnp.concatenate([grad_in_bias[:width], grad_in_bias[2 * width :]])
    bias_sums = sum_all(jnp.concatenate([grad_in_bias, grad_up_bias])[None, :], FC, size)[0]

    xhat_one_rows = row_block(xhat_one, t, chunk)
    inverse_one_rows = row_block(inverse_one, t, chunk)
    tokens_grad_rows = grad_middle + normalise_back(
        grad_norm_one, gain_one, xhat_one_rows, inverse_one_rows
    )
    tokens_grad = tp_gather_rows(to_absolute(tokens_grad_rows.astype(BF)), F32)

    sums = jnp.stack(
        [
            jnp.sum(grad_norm_one * xhat_one_rows, axis=0),
            jnp.sum(grad_norm_one, axis=0),
            jnp.sum(grad_attn.astype(F32), axis=0),
            jnp.sum(grad_norm_two * xhat_rows, axis=0),
            jnp.sum(grad_norm_two, axis=0),
            jnp.sum(cot_rows, axis=0),
        ]
    )
    sums = sum_direct(sums, "tp", tp)
    vector_grads = scatter_sum(sums[:, :half], sums[:, half:], 1)
    return (
        result.reshape(sequences, rows, features),
        tokens_grad.reshape(sequences, rows, features),
        vector_grads[0],
        vector_grads[1],
        in_weight_grad,
        bias_sums[: 2 * width].reshape(2, width),
        out_weight_grad,
        vector_grads[2],
        vector_grads[3],
        vector_grads[4],
        up_grad,
        bias_sums[2 * width :],
        down_grad,
        vector_grads[5],
    )


def solution(mesh):
    in_specs = (
        P("fsdp", "ctx", None),
        P("fsdp", None),
        P(("fsdp", "ctx")),
        P(("fsdp", "ctx")),
        P(None, ("fsdp", "ctx"), "tp"),
        P(None, "tp"),
        P("tp", ("fsdp", "ctx")),
        P(("fsdp", "ctx")),
        P(("fsdp", "ctx")),
        P(("fsdp", "ctx")),
        P(("fsdp", "ctx"), "tp"),
        P("tp"),
        P("tp", ("fsdp", "ctx")),
        P(("fsdp", "ctx")),
        P("fsdp", "ctx", None),
    )
    out_specs = (
        P("fsdp", "ctx", None),
        P("fsdp", "ctx", None),
        P(("fsdp", "ctx")),
        P(("fsdp", "ctx")),
        P(None, ("fsdp", "ctx"), "tp"),
        P(None, "tp"),
        P("tp", ("fsdp", "ctx")),
        P(("fsdp", "ctx")),
        P(("fsdp", "ctx")),
        P(("fsdp", "ctx")),
        P(("fsdp", "ctx"), "tp"),
        P("tp"),
        P("tp", ("fsdp", "ctx")),
        P(("fsdp", "ctx")),
    )
    return jax.shard_map(
        local,
        mesh=mesh,
        in_specs=in_specs,
        out_specs=out_specs,
        check_vma=False,
    )
```
